32 devices in a mesh: term: 8 (over z, core), doc: 4 (over y, x).
Axes of the slice: x: 2, y: 2, z: 4, core: 2. Of those that a mesh axis runs over, the one named last changes fastest.
Arguments:
- tile_values: bfloat16 [384, 512, 128], P('term', 'doc'), may hold values from 0.001 to 1, as said below
- tile_rows: int32 [8, 192], P('term', 'doc'), may hold values from 0 to 15, as said below
- tile_cols: int32 [8, 192], P('term', 'doc'), may hold values from 0 to 15, as said below
- tile_count: int32 [8, 4], P('term', 'doc'), may hold values from 16 to 48, as said below
- start_block: bfloat16 [8192, 256], P('doc'), may hold values from -6 to 6
Outputs:
- row_scale: float32 [16384], P('term')
- col_scale: float32 [8192], P('doc')
- left_basis: bfloat16 [16384, 256], P('term')
- right_basis: bfloat16 [8192, 256], P('doc')
The draws below stay inside these ranges and needn't reach their ends.
Inputs may be any that keep to these rules, and one draw needn't show every extreme that they name: `tile_values`: entries are positive. `tile_rows`: within one block pair the occupied (row, column) pairs are distinct, and every tile row and tile column of every block pair holds an occupied tile. `tile_cols`: paired with tile_rows slot by slot. `tile_count`: some block pair has all 48 slots occupied.
All inputs are finite; a program needn't handle non-finite values.
Results may differ from the reference program's by a relative error of at most 0.006.
The reference program's roundings to bfloat16 on the way count: a program that leaves them out, or rounds other values in their place, can miss the bound.
Values may be sent and summed in bfloat16 or wider, within the bound.
A program may use at most 64 MiB of HBM per device.

```python
import jax
import jax.numpy as jnp
from jax import lax

TILE = 128
K = 256
PASSES = 2
RB = 16
CB = 16
CAP = 48
DOCS = 8192
N_TERM = 8
N_DOC = 4


def draw_tile_values(key, part):
    base = jax.random.fold_in(key, 41)
    entries = jax.random.uniform(base, (N_TERM, CAP, N_DOC, TILE, TILE), jnp.float32, 0.05, 1.0)
    level = jax.random.uniform(jax.random.fold_in(base, 3), (N_TERM, N_DOC), jnp.float32, jnp.log(0.03), 0.0)
    factor = jnp.exp(level)
    scaled = entries * factor[:, None, :, None, None]
    return scaled.reshape(N_TERM * CAP, N_DOC * TILE, TILE).astype(jnp.bfloat16)


def tile_places(key):
    base = jax.random.fold_in(key, 17)
    positions = RB * CB
    scores = jax.random.randint(base, (N_TERM, N_DOC, positions), 0, 1 << 20, dtype=jnp.int32)
    cell = jnp.arange(positions, dtype=jnp.int32)
    row_of = cell // CB
    col_of = cell % CB
    forced = row_of == col_of % RB
    ranked = jnp.where(forced[None, None, :], col_of[None, None, :] - CB, scores * positions + cell[None, None, :])
    order = jnp.argsort(ranked, axis=-1, stable=True)[:, :, :CAP].astype(jnp.int32)
    return (order // CB, order % CB)


def draw_tile_rows(key, part):
    row_part, col_part = tile_places(key)
    return row_part.reshape(N_TERM, N_DOC * CAP)


def draw_tile_cols(key, part):
    row_part, col_part = tile_places(key)
    return col_part.reshape(N_TERM, N_DOC * CAP)


def draw_tile_count(key, part):
    base = jax.random.fold_in(key, 29)
    spread = CAP - CB
    level = jax.random.randint(base, (N_TERM * N_DOC,), 0, spread + 1, dtype=jnp.int32)
    filled = CB + level * level // spread * level // spread
    chosen = jax.random.randint(jax.random.fold_in(base, 1), (), 0, N_TERM * N_DOC, dtype=jnp.int32)
    filled = jnp.where(jnp.arange(N_TERM * N_DOC, dtype=jnp.int32) == chosen, CAP, filled)
    return filled.reshape(N_TERM, N_DOC).astype(jnp.int32)


def block_levels(stream_key, shape, pieces, least, top_value):
    factor_of, own = 1.0, jax.random.fold_in(stream_key, 6)
    for position, parts in pieces:
        draws = jnp.exp(jax.random.uniform(jax.random.fold_in(own, position), (parts,), jnp.float32, least / len(pieces), top_value / len(pieces)))
        factor_of = factor_of * jnp.repeat(draws, shape[position] // parts).reshape([-1 if axis == position else 1 for axis in range(len(shape))])
    return factor_of


def scatter_about(rng, extent, scale, bound, shards=(), kind=jnp.bfloat16):
    loudness = block_levels(rng, extent, shards, -0.22, 0.18) if shards else 1.0
    array = jax.random.normal(rng, extent, jnp.float32) * scale * loudness
    return jnp.minimum(jnp.maximum(array, -bound), bound).astype(kind)


def setup_inputs(seed: int = 0) -> dict:
    arg_keys = jax.random.split(jax.random.key(seed), 6)
    tile_values = draw_tile_values(jax.random.fold_in(arg_keys[5], 71), 0)
    tile_rows = draw_tile_rows(jax.random.fold_in(arg_keys[5], 71), 0)
    tile_cols = draw_tile_cols(jax.random.fold_in(arg_keys[5], 71), 0)
    tile_count = draw_tile_count(jax.random.fold_in(arg_keys[5], 71), 0)
    start_block = scatter_about(arg_keys[4], (DOCS, K), 1.0, 6.0, ((0, 4),))
    return dict(tile_values=tile_values, tile_rows=tile_rows, tile_cols=tile_cols, tile_count=tile_count, start_block=start_block)


PRECISE = lax.Precision.HIGHEST

def factor_inverse(gram):
    lower = jnp.linalg.cholesky(gram)
    identity = jnp.eye(gram.shape[0], dtype=gram.dtype)
    return jax.scipy.linalg.solve_triangular(lower, identity, lower=True).T

def apply_matrix(values, row_ids, col_ids, counts, source, forward):
    width = source.shape[-1]
    if forward:
        out_blocks = RB
    else:
        out_blocks = CB

    def outer_block(outer):

        def inner_step(running, inner):
            if forward:
                term_at, doc_at = (outer, inner)
            else:
                term_at, doc_at = (inner, outer)
            tiles_here = values[term_at, :, doc_at].astype(jnp.float32)
            live_mask = (jnp.arange(CAP, dtype=jnp.int32) < counts[term_at, doc_at]).astype(jnp.float32)
            if forward:
                picked = source[doc_at][col_ids[term_at, doc_at]].astype(jnp.float32)
                product = jnp.einsum('sab,sbk->sak', tiles_here, picked, precision=PRECISE)
                target = row_ids[term_at, doc_at]
            else:
                picked = source[term_at][row_ids[term_at, doc_at]].astype(jnp.float32)
                product = jnp.einsum('sab,sak->sbk', tiles_here, picked, precision=PRECISE)
                target = col_ids[term_at, doc_at]
            product = product * live_mask[:, None, None]
            return (running + jax.ops.segment_sum(product, target, num_segments=out_blocks), None)
        initial = jnp.zeros((out_blocks, TILE, width), jnp.float32)
        inner_total = N_DOC if forward else N_TERM
        return lax.scan(inner_step, initial, jnp.arange(inner_total, dtype=jnp.int32))[0]
    outer_total = N_TERM if forward else N_DOC
    return lax.map(outer_block, jnp.arange(outer_total, dtype=jnp.int32))

def reference(tile_values, tile_rows, tile_cols, tile_count, start_block):
    values = tile_values.reshape(N_TERM, CAP, N_DOC, TILE, TILE)
    row_ids = tile_rows.reshape(N_TERM, N_DOC, CAP).astype(jnp.int32)
    col_ids = tile_cols.reshape(N_TERM, N_DOC, CAP).astype(jnp.int32)
    counts = tile_count.astype(jnp.int32)
    terms_total = N_TERM * RB * TILE
    docs_total = N_DOC * CB * TILE
    col_scale = jnp.ones((N_DOC, CB, TILE, 1), jnp.float32)
    row_scale = jnp.ones((N_TERM, RB, TILE, 1), jnp.float32)
    for sweep_index in range(PASSES):
        row_scale = 1.0 / apply_matrix(values, row_ids, col_ids, counts, col_scale, True)
        col_scale = 1.0 / apply_matrix(values, row_ids, col_ids, counts, row_scale, False)
    row_weight = row_scale * apply_matrix(values, row_ids, col_ids, counts, col_scale, True)
    row_flat = row_scale.reshape(-1, 1)
    col_flat = col_scale.reshape(-1, 1)
    weight_flat = row_weight.reshape(-1)
    start = start_block.astype(jnp.float32)
    start_mean = jnp.sum(start, axis=0)
    scaled_start = (col_flat * start).astype(jnp.bfloat16)
    left_raw = apply_matrix(values, row_ids, col_ids, counts, scaled_start.reshape(N_DOC, CB, TILE, K), True).reshape(-1, K)
    left_block = row_flat * left_raw - weight_flat[:, None] * start_mean[None, :] / docs_total
    left_inverse = factor_inverse(jnp.dot(left_block.T, left_block, precision=PRECISE) / terms_total)
    left_float = jnp.dot(left_block, left_inverse, precision=PRECISE)
    left_basis = left_float.astype(jnp.bfloat16)
    lean = jnp.dot(weight_flat, left_float, precision=PRECISE)
    scaled_left = (row_flat * left_basis.astype(jnp.float32)).astype(jnp.bfloat16)
    right_raw = apply_matrix(values, row_ids, col_ids, counts, scaled_left.reshape(N_TERM, RB, TILE, K), False).reshape(-1, K)
    right_block = col_flat * right_raw - lean[None, :] / docs_total
    right_inverse = factor_inverse(jnp.dot(right_block.T, right_block, precision=PRECISE) / docs_total)
    right_basis = jnp.dot(right_block, right_inverse, precision=PRECISE).astype(jnp.bfloat16)
    return (row_scale.reshape(-1), col_scale.reshape(-1), left_basis, right_basis)
```

```python
import functools

import jax
import jax.numpy as jnp
from jax import lax
from jax.experimental import pallas as pl
from jax.experimental.pallas import tpu as pltpu
from jax.sharding import PartitionSpec as P

TILE = 128
PASSES = 2
RB = 16
CB = 16


PRECISE = lax.Precision.HIGHEST
MESH = pl.DeviceIdType.MESH
VMEM = pl.BlockSpec(memory_space=pltpu.VMEM)
SMEM = pl.BlockSpec(memory_space=pltpu.SMEM)


def factor_inverse(gram):
    lower = jnp.linalg.cholesky(gram)
    identity = jnp.eye(gram.shape[0], dtype=gram.dtype)
    return jax.scipy.linalg.solve_triangular(lower, identity, lower=True).T


def params(identifier):
    return pltpu.CompilerParams(
        collective_id=identifier, has_side_effects=True, vmem_limit_bytes=32 << 20
    )


def greet(axes):
    barrier = pltpu.get_barrier_semaphore()
    total = 0
    for axis in axes:
        n = lax.axis_size(axis)
        me = lax.axis_index(axis)
        for step in range(1, n):
            pl.semaphore_signal(
                barrier, inc=1, device_id={axis: lax.rem(me + step, n)}, device_id_type=MESH
            )
        total += n - 1
    pl.semaphore_wait(barrier, total)


def remote(source, target, send_sem, recv_sem, axis, peer):
    return pltpu.make_async_remote_copy(
        src_ref=source,
        dst_ref=target,
        send_sem=send_sem,
        recv_sem=recv_sem,
        device_id={axis: peer},
        device_id_type=MESH,
    )


def all_sum_kernel(axis, x_ref, o_ref, held, send_sem, recv_sem):
    n = lax.axis_size(axis)
    me = lax.axis_index(axis)
    greet((axis,))
    copies = []
    for step in range(1, n):
        copy = remote(
            x_ref, held.at[step], send_sem.at[step], recv_sem.at[step], axis, lax.rem(me + step, n)
        )
        copy.start()
        copies.append(copy)
    held[0] = x_ref[...]
    for copy in copies:
        copy.wait()
    total = held[me]
    for source in range(1, n):
        total = total + held[lax.rem(me - source + n, n)]
    o_ref[...] = total


def all_sum(x, axis, identifier):
    n = lax.axis_size(axis)
    return pl.pallas_call(
        functools.partial(all_sum_kernel, axis),
        out_shape=jax.ShapeDtypeStruct(x.shape, x.dtype),
        in_specs=[VMEM],
        out_specs=VMEM,
        scratch_shapes=[
            pltpu.VMEM((n,) + x.shape, x.dtype),
            pltpu.SemaphoreType.DMA((n,)),
            pltpu.SemaphoreType.DMA((n,)),
        ],
        compiler_params=params(identifier),
        name="all_sum",
    )(x)


def scatter_sum_kernel(axis, x_ref, o_ref, held, send_sem, recv_sem):
    n = lax.axis_size(axis)
    me = lax.axis_index(axis)
    greet((axis,))
    copies = []
    for step in range(1, n):
        peer = lax.rem(me + step, n)
        copy = remote(
            x_ref.at[peer], held.at[step], send_sem.at[step], recv_sem.at[step], axis, peer
        )
        copy.start()
        copies.append(copy)
    o_ref[...] = x_ref[me]
    for step, copy in enumerate(copies):
        copy.wait()
        o_ref[...] += held[step + 1]


def scatter_sum(x, axis, identifier):
    n = lax.axis_size(axis)
    return pl.pallas_call(
        functools.partial(scatter_sum_kernel, axis),
        out_shape=jax.ShapeDtypeStruct(x.shape[1:], x.dtype),
        in_specs=[VMEM],
        out_specs=VMEM,
        scratch_shapes=[
            pltpu.VMEM(x.shape, x.dtype),
            pltpu.SemaphoreType.DMA((n,)),
            pltpu.SemaphoreType.DMA((n,)),
        ],
        compiler_params=params(identifier),
        name="scatter_sum",
    )(x)


def gather_kernel(axis, x_ref, o_ref, send_sem, recv_sem):
    n = lax.axis_size(axis)
    me = lax.axis_index(axis)
    greet((axis,))
    copies = []
    for step in range(1, n):
        copy = remote(
            x_ref, o_ref.at[me], send_sem.at[step], recv_sem.at[step], axis, lax.rem(me + step, n)
        )
        copy.start()
        copies.append(copy)
    o_ref[me] = x_ref[...]
    for copy in copies:
        copy.wait()


def gather(x, axis, identifier):
    n = lax.axis_size(axis)
    return pl.pallas_call(
        functools.partial(gather_kernel, axis),
        out_shape=jax.ShapeDtypeStruct((n,) + x.shape, x.dtype),
        in_specs=[VMEM],
        out_specs=VMEM,
        scratch_shapes=[
            pltpu.SemaphoreType.DMA((n,)),
            pltpu.SemaphoreType.DMA((n,)),
        ],
        compiler_params=params(identifier),
        name="gather",
    )(x)


def gram_sum_kernel(x_ref, o_ref, first, second, part, done, *sems):
    n, m = lax.axis_size("term"), lax.axis_size("doc")
    me, my = lax.axis_index("term"), lax.axis_index("doc")
    send_a, recv_a, send_b, recv_b, send_c, recv_c = sems
    greet(("term", "doc"))
    copies = []
    for step in range(1, n):
        peer = lax.rem(me + step, n)
        copy = remote(x_ref.at[peer], first.at[step], send_a.at[step], recv_a.at[step], "term", peer)
        copy.start()
        copies.append(copy)
    part[...] = x_ref[me]
    for step, copy in enumerate(copies):
        copy.wait()
        part[...] += first[step + 1]
    copies = []
    for step in range(1, m):
        copy = remote(
            part, second.at[step], send_b.at[step], recv_b.at[step], "doc", lax.rem(my + step, m)
        )
        copy.start()
        copies.append(copy)
    second[0] = part[...]
    for copy in copies:
        copy.wait()
    total = second[my]
    for source in range(1, m):
        total = total + second[lax.rem(my - source + m, m)]
    done[...] = total
    copies = []
    for step in range(1, n):
        copy = remote(
            done, o_ref.at[me], send_c.at[step], recv_c.at[step], "term", lax.rem(me + step, n)
        )
        copy.start()
        copies.append(copy)
    o_ref[me] = done[...]
    for copy in copies:
        copy.wait()


def gram_sum(x, identifier):
    n, m = lax.axis_size("term"), lax.axis_size("doc")
    share = x.shape[1:]
    return pl.pallas_call(
        gram_sum_kernel,
        out_shape=jax.ShapeDtypeStruct(x.shape, x.dtype),
        in_specs=[VMEM],
        out_specs=VMEM,
        scratch_shapes=[
            pltpu.VMEM((n,) + share, x.dtype),
            pltpu.VMEM((m,) + share, x.dtype),
            pltpu.VMEM(share, x.dtype),
            pltpu.VMEM(share, x.dtype),
        ]
        + [pltpu.SemaphoreType.DMA((size,)) for size in (n, n, m, m, n, n)],
        compiler_params=params(identifier),
        name="gram_sum",
    )(x)


def dense_kernel(rows_ref, cols_ref, count_ref, tiles_ref, o_ref):
    def clear(index, carry):
        at = pl.multiple_of(index * 32, 32)
        o_ref[pl.ds(at, 32), :] = jnp.zeros((32, o_ref.shape[1]), o_ref.dtype)
        return carry

    lax.fori_loop(0, o_ref.shape[0] // 32, clear, 0)

    def place(slot, carry):
        row = pl.multiple_of(rows_ref[0, slot] * TILE, TILE)
        col = pl.multiple_of(cols_ref[0, slot] * TILE, TILE)
        o_ref[pl.ds(row, TILE), pl.ds(col, TILE)] = tiles_ref[slot]
        return carry

    lax.fori_loop(0, count_ref[0, 0], place, 0)


def dense_matrix(tile_values, tile_rows, tile_cols, tile_count):
    return pl.pallas_call(
        dense_kernel,
        out_shape=jax.ShapeDtypeStruct((RB * TILE, CB * TILE), tile_values.dtype),
        in_specs=[SMEM, SMEM, SMEM, VMEM],
        out_specs=VMEM,
        compiler_params=pltpu.CompilerParams(vmem_limit_bytes=32 << 20),
        name="dense",
    )(tile_rows, tile_cols, tile_count, tile_values)


def row_sums(matrix, scale):
    return jnp.sum(matrix.astype(jnp.float32) * scale[None, :], axis=1)


def col_sums(matrix, scale):
    return jnp.sum(matrix.astype(jnp.float32) * scale[:, None], axis=0)


def vector_sum(x, axis, identifier):
    return all_sum(x.reshape(-1, TILE), axis, identifier).reshape(-1)


def total_gram(block, extra, scale, identifier):
    n = lax.axis_size("term")
    width = block.shape[1]
    gram = jnp.dot(block.T, block, precision=PRECISE) / scale
    rows = [gram]
    if extra is not None:
        rows += [extra[None, :], jnp.zeros((8 * n - 1, width), jnp.float32)]
    stacked = jnp.concatenate(rows, axis=0) if extra is not None else gram
    summed = gram_sum(stacked.reshape(n, -1, width), identifier).reshape(stacked.shape)
    return summed[:width], (summed[width] if extra is not None else None)


def per_device(tile_values, tile_rows, tile_cols, tile_count, start_block):
    terms_total = RB * TILE * lax.axis_size("term")
    docs_total = CB * TILE * lax.axis_size("doc")
    width = start_block.shape[1]
    matrix = dense_matrix(tile_values, tile_rows, tile_cols, tile_count)

    mean_part = jnp.sum(start_block.astype(jnp.float32), axis=0)
    col_flat = jnp.ones((CB * TILE,), jnp.float32)
    for sweep_index in range(PASSES):
        row_part = row_sums(matrix, col_flat)
        if sweep_index == 0:
            pad = jnp.zeros((8 * TILE - width % (8 * TILE),), jnp.float32)
            joined = vector_sum(jnp.concatenate([row_part, mean_part, pad]), "doc", 0)
            row_total = joined[: RB * TILE]
            start_mean = joined[RB * TILE : RB * TILE + width]
        else:
            row_total = vector_sum(row_part, "doc", 1 + 2 * sweep_index)
        row_flat = 1.0 / row_total
        col_part = col_sums(matrix, row_flat)
        col_flat = 1.0 / vector_sum(col_part, "term", 2 + 2 * sweep_index)
    scaled_start = (col_flat[:, None] * start_block.astype(jnp.float32)).astype(jnp.bfloat16)
    left_part = jnp.dot(matrix, scaled_start, preferred_element_type=jnp.float32)
    doc_size = lax.axis_size("doc")
    left_share = RB * TILE // doc_size
    left_offset = lax.axis_index("doc") * left_share
    weight_sum = vector_sum(row_sums(matrix, col_flat), "doc", 16)
    left_raw = scatter_sum(left_part.reshape(doc_size, left_share, width), "doc", 17)
    row_rows = lax.dynamic_slice_in_dim(row_flat, left_offset, left_share)
    row_weight = row_rows * lax.dynamic_slice_in_dim(weight_sum, left_offset, left_share)
    left_block = (
        row_rows[:, None] * left_raw - row_weight[:, None] * start_mean[None, :] / docs_total
    )
    weighted = jnp.sum(row_weight[:, None] * left_block, axis=0)
    left_gram, weighted = total_gram(left_block, weighted, terms_total, 18)
    left_inverse = factor_inverse(left_gram)
    share_float = jnp.dot(left_block, left_inverse, precision=PRECISE)
    lean = jnp.dot(weighted, left_inverse, precision=PRECISE)
    left_basis = gather(share_float.astype(jnp.bfloat16), "doc", 19).reshape(RB * TILE, width)
    scaled_left = (row_flat[:, None] * left_basis.astype(jnp.float32)).astype(jnp.bfloat16)
    right_part = lax.dot_general(
        matrix, scaled_left, (((0,), (0,)), ((), ())), preferred_element_type=jnp.float32
    )
    term_size = lax.axis_size("term")
    right_share = CB * TILE // term_size
    right_offset = lax.axis_index("term") * right_share
    right_raw = scatter_sum(right_part.reshape(term_size, right_share, width), "term", 20)
    col_rows = lax.dynamic_slice_in_dim(col_flat, right_offset, right_share)
    right_block = col_rows[:, None] * right_raw - lean[None, :] / docs_total
    right_gram, _ = total_gram(right_block, None, docs_total, 21)
    right_inverse = factor_inverse(right_gram)
    right_piece = jnp.dot(right_block, right_inverse, precision=PRECISE).astype(jnp.bfloat16)
    right_basis = gather(right_piece, "term", 22).reshape(CB * TILE, width)
    return (row_flat, col_flat, left_basis, right_basis)


def solution(mesh):
    placed = (
        P("term", "doc", None),
        P("term", "doc"),
        P("term", "doc"),
        P("term", "doc"),
        P("doc", None),
    )
    return jax.shard_map(
        per_device,
        mesh=mesh,
        in_specs=placed,
        out_specs=(P("term"), P("doc"), P("term", None), P("doc", None)),
        check_vma=False,
    )
```

```python
import functools

import jax
import jax.numpy as jnp
from jax import lax
from jax.experimental import pallas as pl
from jax.experimental.pallas import tpu as pltpu
from jax.sharding import PartitionSpec as P

TILE = 128
PASSES = 2
RB = 16
CB = 16


PRECISE = lax.Precision.HIGHEST
MESH = pl.DeviceIdType.MESH
VMEM = pl.BlockSpec(memory_space=pltpu.VMEM)
SMEM = pl.BlockSpec(memory_space=pltpu.SMEM)


BLOCK = 64
GROUP = 8


def block_inverse(block, low, high):
    rows = lax.broadcasted_iota(jnp.int32, block.shape, 0)
    pivots = jnp.ones_like(block)
    for base in range(0, BLOCK, GROUP):
        factors = []
        for at in range(base, base + GROUP):
            column = jnp.broadcast_to(block[:, low + at : low + at + 1], block.shape)
            for past, factor in enumerate(factors):
                column = column - factor * column[base + past : base + past + 1, :]
            pivots = jnp.where(rows == at, column, pivots)
            ratio = column * (1.0 / column[at : at + 1, :])
            factors.append(jnp.where(rows > at, ratio, 0.0))
        for at, factor in enumerate(factors):
            block = block - factor * block[base + at : base + at + 1, :]
    lanes = lax.broadcasted_iota(jnp.int32, block.shape, 1)
    inside = (lanes >= high) & (lanes < high + BLOCK)
    return jnp.where(inside, block * lax.rsqrt(pivots), 0.0)


def inverse_kernel(gram_ref, o_ref, work):
    width = gram_ref.shape[0]
    work[:, :width] = gram_ref[...]
    rows = lax.broadcasted_iota(jnp.int32, (width, width), 0)
    lanes = lax.broadcasted_iota(jnp.int32, (width, width), 1)
    work[:, width:] = jnp.where(rows == lanes, 1.0, 0.0)
    for index in range(width // BLOCK):
        start = index * BLOCK
        near = start // TILE * TILE
        low = start - near
        high = TILE - BLOCK - low
        block = work[start : start + BLOCK, near : near + TILE]
        rows = lax.broadcasted_iota(jnp.int32, block.shape, 0)
        lanes = lax.broadcasted_iota(jnp.int32, block.shape, 1)
        inside = (lanes >= low) & (lanes < low + BLOCK)
        block = jnp.where(inside, block, jnp.where(lanes - high == rows, 1.0, 0.0))
        inverse = block_inverse(block, low, high)
        panel = work[start : start + BLOCK, :]
        solved = jnp.dot(
            inverse,
            jnp.concatenate([panel, panel], axis=0),
            precision=PRECISE,
            preferred_element_type=jnp.float32,
        )
        o_ref[start : start + BLOCK, :] = solved[:, width:]
        if start + BLOCK < width:
            update = lax.dot_general(
                solved[:, :width],
                solved,
                (((0,), (0,)), ((), ())),
                precision=PRECISE,
                preferred_element_type=jnp.float32,
            )
            work[start + BLOCK :, :] = work[start + BLOCK :, :] - update[start + BLOCK :, :]


def factor_inverse(gram):
    width = gram.shape[0]
    return pl.pallas_call(
        inverse_kernel,
        out_shape=jax.ShapeDtypeStruct(gram.shape, gram.dtype),
        in_specs=[VMEM],
        out_specs=VMEM,
        scratch_shapes=[pltpu.VMEM((width, 2 * width), jnp.float32)],
        compiler_params=pltpu.CompilerParams(vmem_limit_bytes=16 << 20),
        name="inverse",
    )(gram).T


def params(identifier):
    return pltpu.CompilerParams(
        collective_id=identifier, has_side_effects=True, vmem_limit_bytes=32 << 20
    )


def greet(axes):
    barrier = pltpu.get_barrier_semaphore()
    total = 0
    for axis in axes:
        n = lax.axis_size(axis)
        me = lax.axis_index(axis)
        for step in range(1, n):
            pl.semaphore_signal(
                barrier, inc=1, device_id={axis: lax.rem(me + step, n)}, device_id_type=MESH
            )
        total += n - 1
    pl.semaphore_wait(barrier, total)


def remote(source, target, send_sem, recv_sem, axis, peer):
    return pltpu.make_async_remote_copy(
        src_ref=source,
        dst_ref=target,
        send_sem=send_sem,
        recv_sem=recv_sem,
        device_id={axis: peer},
        device_id_type=MESH,
    )


def all_sum_kernel(axis, x_ref, o_ref, held, send_sem, recv_sem):
    n = lax.axis_size(axis)
    me = lax.axis_index(axis)
    greet((axis,))
    copies = []
    for step in range(1, n):
        copy = remote(
            x_ref, held.at[step], send_sem.at[step], recv_sem.at[step], axis, lax.rem(me + step, n)
        )
        copy.start()
        copies.append(copy)
    held[0] = x_ref[...]
    for copy in copies:
        copy.wait()
    total = held[me]
    for source in range(1, n):
        total = total + held[lax.rem(me - source + n, n)]
    o_ref[...] = total


def all_sum(x, axis, identifier):
    n = lax.axis_size(axis)
    return pl.pallas_call(
        functools.partial(all_sum_kernel, axis),
        out_shape=jax.ShapeDtypeStruct(x.shape, x.dtype),
        in_specs=[VMEM],
        out_specs=VMEM,
        scratch_shapes=[
            pltpu.VMEM((n,) + x.shape, x.dtype),
            pltpu.SemaphoreType.DMA((n,)),
            pltpu.SemaphoreType.DMA((n,)),
        ],
        compiler_params=params(identifier),
        name="all_sum",
    )(x)


def scatter_sum_kernel(axis, x_ref, o_ref, held, send_sem, recv_sem):
    n = lax.axis_size(axis)
    me = lax.axis_index(axis)
    greet((axis,))
    copies = []
    for step in range(1, n):
        peer = lax.rem(me + step, n)
        copy = remote(
            x_ref.at[peer], held.at[step], send_sem.at[step], recv_sem.at[step], axis, peer
        )
        copy.start()
        copies.append(copy)
    o_ref[...] = x_ref[me]
    for step, copy in enumerate(copies):
        copy.wait()
        o_ref[...] += held[step + 1]


def scatter_sum(x, axis, identifier):
    n = lax.axis_size(axis)
    return pl.pallas_call(
        functools.partial(scatter_sum_kernel, axis),
        out_shape=jax.ShapeDtypeStruct(x.shape[1:], x.dtype),
        in_specs=[VMEM],
        out_specs=VMEM,
        scratch_shapes=[
            pltpu.VMEM(x.shape, x.dtype),
            pltpu.SemaphoreType.DMA((n,)),
            pltpu.SemaphoreType.DMA((n,)),
        ],
        compiler_params=params(identifier),
        name="scatter_sum",
    )(x)


def gather_kernel(axis, x_ref, o_ref, send_sem, recv_sem):
    n = lax.axis_size(axis)
    me = lax.axis_index(axis)
    greet((axis,))
    copies = []
    for step in range(1, n):
        copy = remote(
            x_ref, o_ref.at[me], send_sem.at[step], recv_sem.at[step], axis, lax.rem(me + step, n)
        )
        copy.start()
        copies.append(copy)
    o_ref[me] = x_ref[...]
    for copy in copies:
        copy.wait()


def gather(x, axis, identifier):
    n = lax.axis_size(axis)
    return pl.pallas_call(
        functools.partial(gather_kernel, axis),
        out_shape=jax.ShapeDtypeStruct((n,) + x.shape, x.dtype),
        in_specs=[VMEM],
        out_specs=VMEM,
        scratch_shapes=[
            pltpu.SemaphoreType.DMA((n,)),
            pltpu.SemaphoreType.DMA((n,)),
        ],
        compiler_params=params(identifier),
        name="gather",
    )(x)


def gram_sum_kernel(x_ref, o_ref, first, second, part, done, *sems):
    n, m = lax.axis_size("term"), lax.axis_size("doc")
    me, my = lax.axis_index("term"), lax.axis_index("doc")
    send_a, recv_a, send_b, recv_b, send_c, recv_c = sems
    greet(("term", "doc"))
    copies = []
    for step in range(1, n):
        peer = lax.rem(me + step, n)
        copy = remote(x_ref.at[peer], first.at[step], send_a.at[step], recv_a.at[step], "term", peer)
        copy.start()
        copies.append(copy)
    part[...] = x_ref[me]
    for step, copy in enumerate(copies):
        copy.wait()
        part[...] += first[step + 1]
    copies = []
    for step in range(1, m):
        copy = remote(
            part, second.at[step], send_b.at[step], recv_b.at[step], "doc", lax.rem(my + step, m)
        )
        copy.start()
        copies.append(copy)
    second[0] = part[...]
    for copy in copies:
        copy.wait()
    total = second[my]
    for source in range(1, m):
        total = total + second[lax.rem(my - source + m, m)]
    done[...] = total
    copies = []
    for step in range(1, n):
        copy = remote(
            done, o_ref.at[me], send_c.at[step], recv_c.at[step], "term", lax.rem(me + step, n)
        )
        copy.start()
        copies.append(copy)
    o_ref[me] = done[...]
    for copy in copies:
        copy.wait()


def gram_sum(x, identifier):
    n, m = lax.axis_size("term"), lax.axis_size("doc")
    share = x.shape[1:]
    return pl.pallas_call(
        gram_sum_kernel,
        out_shape=jax.ShapeDtypeStruct(x.shape, x.dtype),
        in_specs=[VMEM],
        out_specs=VMEM,
        scratch_shapes=[
            pltpu.VMEM((n,) + share, x.dtype),
            pltpu.VMEM((m,) + share, x.dtype),
            pltpu.VMEM(share, x.dtype),
            pltpu.VMEM(share, x.dtype),
        ]
        + [pltpu.SemaphoreType.DMA((size,)) for size in (n, n, m, m, n, n)],
        compiler_params=params(identifier),
        name="gram_sum",
    )(x)


def dense_kernel(rows_ref, cols_ref, count_ref, tiles_ref, o_ref, t_ref):
    def clear(index, carry):
        at = pl.multiple_of(index * 32, 32)
        o_ref[pl.ds(at, 32), :] = jnp.zeros((32, o_ref.shape[1]), o_ref.dtype)
        t_ref[pl.ds(at, 32), :] = jnp.zeros((32, t_ref.shape[1]), t_ref.dtype)
        return carry

    lax.fori_loop(0, o_ref.shape[0] // 32, clear, 0)

    def place(slot, carry):
        row = pl.multiple_of(rows_ref[0, slot] * TILE, TILE)
        col = pl.multiple_of(cols_ref[0, slot] * TILE, TILE)
        tile = tiles_ref[slot]
        o_ref[pl.ds(row, TILE), pl.ds(col, TILE)] = tile
        t_ref[pl.ds(col, TILE), pl.ds(row, TILE)] = tile.T
        return carry

    lax.fori_loop(0, count_ref[0, 0], place, 0)


def dense_matrix(tile_values, tile_rows, tile_cols, tile_count):
    return pl.pallas_call(
        dense_kernel,
        out_shape=[
            jax.ShapeDtypeStruct((RB * TILE, CB * TILE), tile_values.dtype),
            jax.ShapeDtypeStruct((CB * TILE, RB * TILE), tile_values.dtype),
        ],
        in_specs=[SMEM, SMEM, SMEM, VMEM],
        out_specs=[VMEM, VMEM],
        compiler_params=pltpu.CompilerParams(vmem_limit_bytes=32 << 20),
        name="dense",
    )(tile_rows, tile_cols, tile_count, tile_values)


def row_sums(matrix, scale):
    return jnp.sum(matrix.astype(jnp.float32) * scale[None, :], axis=1)


def col_sums(matrix, scale):
    return jnp.sum(matrix.astype(jnp.float32) * scale[:, None], axis=0)


def vector_sum(x, axis, identifier):
    return all_sum(x.reshape(-1, TILE), axis, identifier).reshape(-1)


def total_gram(block, extra, scale, identifier):
    n = lax.axis_size("term")
    width = block.shape[1]
    gram = jnp.dot(block.T, block, precision=PRECISE) / scale
    rows = [gram]
    if extra is not None:
        rows += [extra[None, :], jnp.zeros((8 * n - 1, width), jnp.float32)]
    stacked = jnp.concatenate(rows, axis=0) if extra is not None else gram
    summed = gram_sum(stacked.reshape(n, -1, width), identifier).reshape(stacked.shape)
    return summed[:width], (summed[width] if extra is not None else None)


def per_device(tile_values, tile_rows, tile_cols, tile_count, start_block):
    terms_total = RB * TILE * lax.axis_size("term")
    docs_total = CB * TILE * lax.axis_size("doc")
    width = start_block.shape[1]
    matrix, turned = dense_matrix(tile_values, tile_rows, tile_cols, tile_count)

    mean_part = jnp.sum(start_block.astype(jnp.float32), axis=0)
    col_flat = jnp.ones((CB * TILE,), jnp.float32)
    for sweep_index in range(PASSES):
        row_part = row_sums(matrix, col_flat)
        if sweep_index == 0:
            pad = jnp.zeros((8 * TILE - width % (8 * TILE),), jnp.float32)
            joined = vector_sum(jnp.concatenate([row_part, mean_part, pad]), "doc", 0)
            row_total = joined[: RB * TILE]
            start_mean = joined[RB * TILE : RB * TILE + width]
        else:
            row_total = vector_sum(row_part, "doc", 1 + 2 * sweep_index)
        row_flat = 1.0 / row_total
        col_part = col_sums(matrix, row_flat)
        col_flat = 1.0 / vector_sum(col_part, "term", 2 + 2 * sweep_index)
    scaled_start = (col_flat[:, None] * start_block.astype(jnp.float32)).astype(jnp.bfloat16)
    left_part = jnp.dot(matrix, scaled_start, preferred_element_type=jnp.float32)
    doc_size = lax.axis_size("doc")
    left_share = RB * TILE // doc_size
    left_offset = lax.axis_index("doc") * left_share
    weight_sum = vector_sum(row_sums(matrix, col_flat), "doc", 16)
    left_raw = scatter_sum(left_part.reshape(doc_size, left_share, width), "doc", 17)
    row_rows = lax.dynamic_slice_in_dim(row_flat, left_offset, left_share)
    row_weight = row_rows * lax.dynamic_slice_in_dim(weight_sum, left_offset, left_share)
    left_block = (
        row_rows[:, None] * left_raw - row_weight[:, None] * start_mean[None, :] / docs_total
    )
    weighted = jnp.sum(row_weight[:, None] * left_block, axis=0)
    left_gram, weighted = total_gram(left_block, weighted, terms_total, 18)
    left_inverse = factor_inverse(left_gram)
    share_float = jnp.dot(left_block, left_inverse, precision=PRECISE)
    lean = jnp.dot(weighted, left_inverse, precision=PRECISE)
    left_basis = gather(share_float.astype(jnp.bfloat16), "doc", 19).reshape(RB * TILE, width)
    scaled_left = (row_flat[:, None] * left_basis.astype(jnp.float32)).astype(jnp.bfloat16)
    right_part = jnp.dot(turned, scaled_left, preferred_element_type=jnp.float32)
    term_size = lax.axis_size("term")
    right_share = CB * TILE // term_size
    right_offset = lax.axis_index("term") * right_share
    right_raw = scatter_sum(right_part.reshape(term_size, right_share, width), "term", 20)
    col_rows = lax.dynamic_slice_in_dim(col_flat, right_offset, right_share)
    right_block = col_rows[:, None] * right_raw - lean[None, :] / docs_total
    right_gram, _ = total_gram(right_block, None, docs_total, 21)
    right_inverse = factor_inverse(right_gram)
    right_piece = jnp.dot(right_block, right_inverse, precision=PRECISE).astype(jnp.bfloat16)
    right_basis = gather(right_piece, "term", 22).reshape(CB * TILE, width)
    return (row_flat, col_flat, left_basis, right_basis)


def solution(mesh):
    placed = (
        P("term", "doc", None),
        P("term", "doc"),
        P("term", "doc"),
        P("term", "doc"),
        P("doc", None),
    )
    return jax.shard_map(
        per_device,
        mesh=mesh,
        in_specs=placed,
        out_specs=(P("term"), P("doc"), P("term", None), P("doc", None)),
        check_vma=False,
    )
```

```python
import functools

import jax
import jax.numpy as jnp
from jax import lax
from jax.experimental import pallas as pl
from jax.experimental.pallas import tpu as pltpu
from jax.sharding import PartitionSpec as P

TILE = 128
PASSES = 2
RB = 16
CB = 16


PRECISE = lax.Precision.HIGHEST
MESH = pl.DeviceIdType.MESH
VMEM = pl.BlockSpec(memory_space=pltpu.VMEM)
SMEM = pl.BlockSpec(memory_space=pltpu.SMEM)


BLOCK = 64
GROUP = 8


def block_inverse(block, low, high):
    rows = lax.broadcasted_iota(jnp.int32, block.shape, 0)
    pivots = jnp.ones_like(block)
    for base in range(0, BLOCK, GROUP):
        factors = []
        for at in range(base, base + GROUP):
            column = jnp.broadcast_to(block[:, low + at : low + at + 1], block.shape)
            for past, factor in enumerate(factors):
                column = column - factor * column[base + past : base + past + 1, :]
            pivots = jnp.where(rows == at, column, pivots)
            ratio = column * (1.0 / column[at : at + 1, :])
            factors.append(jnp.where(rows > at, ratio, 0.0))
        for at, factor in enumerate(factors):
            block = block - factor * block[base + at : base + at + 1, :]
    lanes = lax.broadcasted_iota(jnp.int32, block.shape, 1)
    inside = (lanes >= high) & (lanes < high + BLOCK)
    return jnp.where(inside, block * lax.rsqrt(pivots), 0.0)


def inverse_kernel(gram_ref, o_ref, work):
    width = gram_ref.shape[0]
    work[:, :width] = gram_ref[...]
    rows = lax.broadcasted_iota(jnp.int32, (width, width), 0)
    lanes = lax.broadcasted_iota(jnp.int32, (width, width), 1)
    work[:, width:] = jnp.where(rows == lanes, 1.0, 0.0)
    for index in range(width // BLOCK):
        start = index * BLOCK
        near = start // TILE * TILE
        low = start - near
        high = TILE - BLOCK - low
        block = work[start : start + BLOCK, near : near + TILE]
        rows = lax.broadcasted_iota(jnp.int32, block.shape, 0)
        lanes = lax.broadcasted_iota(jnp.int32, block.shape, 1)
        inside = (lanes >= low) & (lanes < low + BLOCK)
        block = jnp.where(inside, block, jnp.where(lanes - high == rows, 1.0, 0.0))
        inverse = block_inverse(block, low, high)
        panel = work[start : start + BLOCK, :]
        solved = jnp.dot(
            inverse,
            jnp.concatenate([panel, panel], axis=0),
            precision=PRECISE,
            preferred_element_type=jnp.float32,
        )
        o_ref[start : start + BLOCK, :] = solved[:, width:]
        if start + BLOCK < width:
            update = lax.dot_general(
                solved[:, :width],
                solved,
                (((0,), (0,)), ((), ())),
                precision=PRECISE,
                preferred_element_type=jnp.float32,
            )
            work[start + BLOCK :, :] = work[start + BLOCK :, :] - update[start + BLOCK :, :]


def factor_inverse(gram):
    width = gram.shape[0]
    return pl.pallas_call(
        inverse_kernel,
        out_shape=jax.ShapeDtypeStruct(gram.shape, gram.dtype),
        in_specs=[VMEM],
        out_specs=VMEM,
        scratch_shapes=[pltpu.VMEM((width, 2 * width), jnp.float32)],
        compiler_params=pltpu.CompilerParams(vmem_limit_bytes=16 << 20),
        name="inverse",
    )(gram).T


def params(identifier):
    return pltpu.CompilerParams(
        collective_id=identifier, has_side_effects=True, vmem_limit_bytes=32 << 20
    )


def greet(axes):
    barrier = pltpu.get_barrier_semaphore()
    total = 0
    for axis in axes:
        n = lax.axis_size(axis)
        me = lax.axis_index(axis)
        for step in range(1, n):
            pl.semaphore_signal(
                barrier, inc=1, device_id={axis: lax.rem(me + step, n)}, device_id_type=MESH
            )
        total += n - 1
    pl.semaphore_wait(barrier, total)


def remote(source, target, send_sem, recv_sem, axis, peer):
    return pltpu.make_async_remote_copy(
        src_ref=source,
        dst_ref=target,
        send_sem=send_sem,
        recv_sem=recv_sem,
        device_id={axis: peer},
        device_id_type=MESH,
    )


def all_sum_kernel(axis, x_ref, o_ref, held, send_sem, recv_sem):
    n = lax.axis_size(axis)
    me = lax.axis_index(axis)
    greet((axis,))
    copies = []
    for step in range(1, n):
        copy = remote(
            x_ref, held.at[step], send_sem.at[step], recv_sem.at[step], axis, lax.rem(me + step, n)
        )
        copy.start()
        copies.append(copy)
    held[0] = x_ref[...]
    for copy in copies:
        copy.wait()
    total = held[me]
    for source in range(1, n):
        total = total + held[lax.rem(me - source + n, n)]
    o_ref[...] = total


def all_sum(x, axis, identifier):
    n = lax.axis_size(axis)
    return pl.pallas_call(
        functools.partial(all_sum_kernel, axis),
        out_shape=jax.ShapeDtypeStruct(x.shape, x.dtype),
        in_specs=[VMEM],
        out_specs=VMEM,
        scratch_shapes=[
            pltpu.VMEM((n,) + x.shape, x.dtype),
            pltpu.SemaphoreType.DMA((n,)),
            pltpu.SemaphoreType.DMA((n,)),
        ],
        compiler_params=params(identifier),
        name="all_sum",
    )(x)


def scatter_sum_kernel(axis, x_ref, o_ref, held, send_sem, recv_sem):
    n = lax.axis_size(axis)
    me = lax.axis_index(axis)
    greet((axis,))
    copies = []
    for step in range(1, n):
        peer = lax.rem(me + step, n)
        copy = remote(
            x_ref.at[peer], held.at[step], send_sem.at[step], recv_sem.at[step], axis, peer
        )
        copy.start()
        copies.append(copy)
    o_ref[...] = x_ref[me]
    for step, copy in enumerate(copies):
        copy.wait()
        o_ref[...] += held[step + 1]


def scatter_sum(x, axis, identifier):
    n = lax.axis_size(axis)
    return pl.pallas_call(
        functools.partial(scatter_sum_kernel, axis),
        out_shape=jax.ShapeDtypeStruct(x.shape[1:], x.dtype),
        in_specs=[VMEM],
        out_specs=VMEM,
        scratch_shapes=[
            pltpu.VMEM(x.shape, x.dtype),
            pltpu.SemaphoreType.DMA((n,)),
            pltpu.SemaphoreType.DMA((n,)),
        ],
        compiler_params=params(identifier),
        name="scatter_sum",
    )(x)


def gather_kernel(axis, x_ref, o_ref, send_sem, recv_sem):
    n = lax.axis_size(axis)
    me = lax.axis_index(axis)
    greet((axis,))
    copies = []
    for step in range(1, n):
        copy = remote(
            x_ref, o_ref.at[me], send_sem.at[step], recv_sem.at[step], axis, lax.rem(me + step, n)
        )
        copy.start()
        copies.append(copy)
    o_ref[me] = x_ref[...]
    for copy in copies:
        copy.wait()


def gather(x, axis, identifier):
    n = lax.axis_size(axis)
    return pl.pallas_call(
        functools.partial(gather_kernel, axis),
        out_shape=jax.ShapeDtypeStruct((n,) + x.shape, x.dtype),
        in_specs=[VMEM],
        out_specs=VMEM,
        scratch_shapes=[
            pltpu.SemaphoreType.DMA((n,)),
            pltpu.SemaphoreType.DMA((n,)),
        ],
        compiler_params=params(identifier),
        name="gather",
    )(x)


def paired():
    n, me = lax.axis_size("term"), lax.axis_index("term")
    return n // 2, me // 2, lax.rem(me, 2)


def greet_paired(with_doc):
    nz, z, c = paired()
    barrier = pltpu.get_barrier_semaphore()
    targets = [("term", 2 * z + 1 - c)]
    targets += [("term", 2 * lax.rem(z + step, nz) + c) for step in range(1, nz)]
    if with_doc:
        m, my = lax.axis_size("doc"), lax.axis_index("doc")
        targets += [("doc", lax.rem(my + step, m)) for step in range(1, m)]
    for axis, peer in targets:
        pl.semaphore_signal(barrier, inc=1, device_id={axis: peer}, device_id_type=MESH)
    pl.semaphore_wait(barrier, len(targets))


def scatter_paired(x_ref, near, mid, far, total_ref, near_send, near_recv, far_send, far_recv):
    nz, z, c = paired()
    order = list(range(1, nz)) + [0]
    near_copies = {}
    for step in order:
        near_copies[step] = remote(
            x_ref.at[lax.rem(z + step, nz), 1 - c],
            near.at[step],
            near_send.at[step],
            near_recv.at[step],
            "term",
            2 * z + 1 - c,
        )
        near_copies[step].start()
    far_copies = []
    for step in range(1, nz):
        near_copies[step].wait()
        there = lax.rem(z + step, nz)
        mid[step] = x_ref[there, c] + near[step]
        copy = remote(
            mid.at[step], far.at[step], far_send.at[step], far_recv.at[step], "term", 2 * there + c
        )
        copy.start()
        far_copies.append(copy)
    near_copies[0].wait()
    total_ref[...] = x_ref[z, c] + near[0]
    for step, copy in enumerate(far_copies):
        copy.wait()
        total_ref[...] += far[step + 1]


def gather_paired(x_ref, o_ref, near_send, near_recv, far_send, far_recv):
    nz, z, c = paired()
    sibling = 2 * z + 1 - c
    far_copies = []
    for step in range(1, nz):
        copy = remote(
            x_ref,
            o_ref.at[z, c],
            far_send.at[step],
            far_recv.at[step],
            "term",
            2 * lax.rem(z + step, nz) + c,
        )
        copy.start()
        far_copies.append(copy)
    copy = remote(x_ref, o_ref.at[z, c], near_send.at[0], near_recv.at[0], "term", sibling)
    copy.start()
    near_copies = [copy]
    o_ref[z, c] = x_ref[...]
    for step in range(1, nz):
        far_copies[step - 1].wait()
        here = o_ref.at[lax.rem(z - step + nz, nz), c]
        copy = remote(here, here, near_send.at[step], near_recv.at[step], "term", sibling)
        copy.start()
        near_copies.append(copy)
    for copy in near_copies:
        copy.wait()


def semaphores(*sizes):
    return [pltpu.SemaphoreType.DMA((size,)) for size in sizes]


def scatter_term_kernel(x_ref, o_ref, near, mid, far, *sems):
    greet_paired(False)
    scatter_paired(x_ref, near, mid, far, o_ref, *sems)


def scatter_term(x, identifier):
    nz = x.shape[0]
    share = x.shape[2:]
    return pl.pallas_call(
        scatter_term_kernel,
        out_shape=jax.ShapeDtypeStruct(share, x.dtype),
        in_specs=[VMEM],
        out_specs=VMEM,
        scratch_shapes=[pltpu.VMEM((nz,) + share, x.dtype)] * 3 + semaphores(nz, nz, nz, nz),
        compiler_params=params(identifier),
        name="scatter_term",
    )(x)


def gather_term_kernel(x_ref, o_ref, *sems):
    greet_paired(False)
    gather_paired(x_ref, o_ref, *sems)


def gather_term(x, identifier):
    nz = lax.axis_size("term") // 2
    return pl.pallas_call(
        gather_term_kernel,
        out_shape=jax.ShapeDtypeStruct((nz, 2) + x.shape, x.dtype),
        in_specs=[VMEM],
        out_specs=VMEM,
        scratch_shapes=semaphores(nz, nz, nz, nz),
        compiler_params=params(identifier),
        name="gather_term",
    )(x)


def gram_sum_kernel(x_ref, o_ref, near, mid, far, second, part, done, *sems):
    m, my = lax.axis_size("doc"), lax.axis_index("doc")
    send_b, recv_b = sems[4:6]
    greet_paired(True)
    scatter_paired(x_ref, near, mid, far, part, *sems[:4])
    copies = []
    for step in range(1, m):
        copy = remote(
            part, second.at[step], send_b.at[step], recv_b.at[step], "doc", lax.rem(my + step, m)
        )
        copy.start()
        copies.append(copy)
    second[0] = part[...]
    for copy in copies:
        copy.wait()
    total = second[my]
    for source in range(1, m):
        total = total + second[lax.rem(my - source + m, m)]
    done[...] = total
    gather_paired(done, o_ref, *sems[6:])


def gram_sum(x, identifier):
    nz, m = x.shape[0], lax.axis_size("doc")
    share = x.shape[2:]
    return pl.pallas_call(
        gram_sum_kernel,
        out_shape=jax.ShapeDtypeStruct(x.shape, x.dtype),
        in_specs=[VMEM],
        out_specs=VMEM,
        scratch_shapes=[pltpu.VMEM((nz,) + share, x.dtype)] * 3
        + [
            pltpu.VMEM((m,) + share, x.dtype),
            pltpu.VMEM(share, x.dtype),
            pltpu.VMEM(share, x.dtype),
        ]
        + semaphores(nz, nz, nz, nz, m, m, nz, nz, nz, nz),
        compiler_params=params(identifier),
        name="gram_sum",
    )(x)


def dense_kernel(rows_ref, cols_ref, count_ref, tiles_ref, o_ref, t_ref):
    def clear(index, carry):
        at = pl.multiple_of(index * 32, 32)
        o_ref[pl.ds(at, 32), :] = jnp.zeros((32, o_ref.shape[1]), o_ref.dtype)
        t_ref[pl.ds(at, 32), :] = jnp.zeros((32, t_ref.shape[1]), t_ref.dtype)
        return carry

    lax.fori_loop(0, o_ref.shape[0] // 32, clear, 0)

    def place(slot, carry):
        row = pl.multiple_of(rows_ref[0, slot] * TILE, TILE)
        col = pl.multiple_of(cols_ref[0, slot] * TILE, TILE)
        tile = tiles_ref[slot]
        o_ref[pl.ds(row, TILE), pl.ds(col, TILE)] = tile
        t_ref[pl.ds(col, TILE), pl.ds(row, TILE)] = tile.T
        return carry

    lax.fori_loop(0, count_ref[0, 0], place, 0)


def dense_matrix(tile_values, tile_rows, tile_cols, tile_count):
    return pl.pallas_call(
        dense_kernel,
        out_shape=[
            jax.ShapeDtypeStruct((RB * TILE, CB * TILE), tile_values.dtype),
            jax.ShapeDtypeStruct((CB * TILE, RB * TILE), tile_values.dtype),
        ],
        in_specs=[SMEM, SMEM, SMEM, VMEM],
        out_specs=[VMEM, VMEM],
        compiler_params=pltpu.CompilerParams(vmem_limit_bytes=32 << 20),
        name="dense",
    )(tile_rows, tile_cols, tile_count, tile_values)


def row_sums(matrix, scale):
    return jnp.sum(matrix.astype(jnp.float32) * scale[None, :], axis=1)


def col_sums(matrix, scale):
    return jnp.sum(matrix.astype(jnp.float32) * scale[:, None], axis=0)


def vector_sum(x, axis, identifier):
    return all_sum(x.reshape(-1, TILE), axis, identifier).reshape(-1)


def total_gram(block, extra, scale, identifier):
    n = lax.axis_size("term")
    width = block.shape[1]
    gram = jnp.dot(block.T, block, precision=PRECISE) / scale
    rows = [gram]
    if extra is not None:
        rows += [extra[None, :], jnp.zeros((8 * n - 1, width), jnp.float32)]
    stacked = jnp.concatenate(rows, axis=0) if extra is not None else gram
    summed = gram_sum(stacked.reshape(n // 2, 2, -1, width), identifier).reshape(stacked.shape)
    return summed[:width], (summed[width] if extra is not None else None)


def per_device(tile_values, tile_rows, tile_cols, tile_count, start_block):
    terms_total = RB * TILE * lax.axis_size("term")
    docs_total = CB * TILE * lax.axis_size("doc")
    width = start_block.shape[1]
    matrix, turned = dense_matrix(tile_values, tile_rows, tile_cols, tile_count)

    mean_part = jnp.sum(start_block.astype(jnp.float32), axis=0)
    col_flat = jnp.ones((CB * TILE,), jnp.float32)
    for sweep_index in range(PASSES):
        row_part = row_sums(matrix, col_flat)
        if sweep_index == 0:
            pad = jnp.zeros((8 * TILE - width % (8 * TILE),), jnp.float32)
            joined = vector_sum(jnp.concatenate([row_part, mean_part, pad]), "doc", 0)
            row_total = joined[: RB * TILE]
            start_mean = joined[RB * TILE : RB * TILE + width]
        else:
            row_total = vector_sum(row_part, "doc", 1 + 2 * sweep_index)
        row_flat = 1.0 / row_total
        col_part = col_sums(matrix, row_flat)
        col_flat = 1.0 / vector_sum(col_part, "term", 2 + 2 * sweep_index)
    scaled_start = (col_flat[:, None] * start_block.astype(jnp.float32)).astype(jnp.bfloat16)
    left_part = jnp.dot(matrix, scaled_start, preferred_element_type=jnp.float32)
    doc_size = lax.axis_size("doc")
    left_share = RB * TILE // doc_size
    left_offset = lax.axis_index("doc") * left_share
    weight_sum = vector_sum(row_sums(matrix, col_flat), "doc", 16)
    left_raw = scatter_sum(left_part.reshape(doc_size, left_share, width), "doc", 17)
    row_rows = lax.dynamic_slice_in_dim(row_flat, left_offset, left_share)
    row_weight = row_rows * lax.dynamic_slice_in_dim(weight_sum, left_offset, left_share)
    left_block = (
        row_rows[:, None] * left_raw - row_weight[:, None] * start_mean[None, :] / docs_total
    )
    weighted = jnp.sum(row_weight[:, None] * left_block, axis=0)
    left_gram, weighted = total_gram(left_block, weighted, terms_total, 18)
    left_inverse = factor_inverse(left_gram)
    share_float = jnp.dot(left_block, left_inverse, precision=PRECISE)
    lean = jnp.dot(weighted, left_inverse, precision=PRECISE)
    left_basis = gather(share_float.astype(jnp.bfloat16), "doc", 19).reshape(RB * TILE, width)
    scaled_left = (row_flat[:, None] * left_basis.astype(jnp.float32)).astype(jnp.bfloat16)
    right_part = jnp.dot(turned, scaled_left, preferred_element_type=jnp.float32)
    term_size = lax.axis_size("term")
    right_share = CB * TILE // term_size
    right_offset = lax.axis_index("term") * right_share
    right_raw = scatter_term(right_part.reshape(term_size // 2, 2, right_share, width), 20)
    col_rows = lax.dynamic_slice_in_dim(col_flat, right_offset, right_share)
    right_block = col_rows[:, None] * right_raw - lean[None, :] / docs_total
    right_gram, _ = total_gram(right_block, None, docs_total, 21)
    right_inverse = factor_inverse(right_gram)
    right_piece = jnp.dot(right_block, right_inverse, precision=PRECISE).astype(jnp.bfloat16)
    right_basis = gather_term(right_piece, 22).reshape(CB * TILE, width)
    return (row_flat, col_flat, left_basis, right_basis)


def solution(mesh):
    placed = (
        P("term", "doc", None),
        P("term", "doc"),
        P("term", "doc"),
        P("term", "doc"),
        P("doc", None),
    )
    return jax.shard_map(
        per_device,
        mesh=mesh,
        in_specs=placed,
        out_specs=(P("term"), P("doc"), P("term", None), P("doc", None)),
        check_vma=False,
    )
```
